32 devices in a mesh: row: 4 (over x, core), col: 8 (over z, y).
Axes of the slice: x: 2, y: 2, z: 4, core: 2. Of those that a mesh axis runs over, the one named last changes fastest.
Arguments:
- right_sides: float32 [3, 4, 512, 64], P(None, None, 'row'), may hold values from -6 to 6
- diag_inverse: float32 [3, 4, 512, 512], replicated, as said below
- sub_blocks: float32 [3, 4, 4, 512, 512], P(None, None, None, 'row', 'col'), may hold values from -0.125 to 0.125
- block_mask: int32 [3, 4, 4], replicated, may hold values 0 or 1
- anc_values: float32 [2, 4, 512, 512], P(None, None, 'row', 'col'), may hold values from -0.09375 to 0.09375
- anc_rows: int32 [2, 4, 512], P(None, None, 'row'), may hold values from 0 to 2047, as said below
- anc_count: int32 [2, 4], replicated, may hold values from 256 to 512, as said below
- far_factor: float32 [4, 512, 32768], P(None, 'col', 'row'), may hold values from -0.1875 to 0.1875
- far_rhs: float32 [32768, 64], P(('row', 'col')), may hold values from -6 to 6
- far_solution: float32 [32768, 64], P('row'), may hold values from -4 to 4
Outputs:
- forward_solution: float32 [3, 4, 512, 64], P(None, None, 'row')
- solution: float32 [3, 4, 512, 64], P(None, None, 'row')
- far_update: float32 [32768, 64], P(('row', 'col'))
The draws below stay inside these ranges and needn't reach their ends.
Inputs may be any that keep to these rules, and one draw needn't show every extreme that they name: `diag_inverse`: each diagonal-block inverse is lower triangular. `anc_rows`: each list holds distinct rows of the parent's window in ascending order; entries at positions anc_count or later are not used. `anc_count`: some list is full and some holds exactly 256 live entries in every draw. `block_mask`: entries on and above the block diagonal are not used.
All inputs are finite; a program needn't handle non-finite values.
Results may differ from the reference program's by a relative error of at most 0.0001.
Values sent between devices are 32-bit elements; how exact they have to be, the bound alone decides.
A program may use at most 128 MiB of HBM per device.

```python
import jax
import jax.numpy as jnp
from jax import lax

PW = 512
NPAN = 4
RHS = 64
W = 2048
ANC = 512
R_FAR = 32768


def draw_diag_inverse(key, part):
    first, second = jax.random.split(key)
    shape = (3, NPAN, PW, PW)
    below = jax.random.normal(first, shape, jnp.float32) * (0.6 / PW ** 0.5)
    middle = jax.random.uniform(second, (3, NPAN, PW), jnp.float32, 0.8, 1.25)
    lower = jnp.tril(jnp.ones((PW, PW), jnp.float32), -1)
    return below * lower + middle[..., None] * jnp.eye(PW, dtype=jnp.float32)


def draw_anc_rows(key, part):
    keys = jax.random.split(jax.random.fold_in(key, 3), 2 * NPAN)
    chosen = jax.vmap(lambda one_key: jax.random.permutation(one_key, NPAN * PW)[:ANC])(keys)
    return jnp.sort(chosen, axis=1).reshape(2, NPAN, ANC).astype(jnp.int32)


def draw_anc_count(key, part):
    counts = jax.random.randint(jax.random.fold_in(key, 5), (2 * NPAN,), ANC // 2, ANC + 1)
    fullest = jax.random.randint(jax.random.fold_in(key, 11), (), 0, 2 * NPAN)
    offset = jax.random.randint(jax.random.fold_in(key, 13), (), 1, 2 * NPAN)
    emptiest = (fullest + offset) % (2 * NPAN)
    positions = jnp.arange(2 * NPAN)
    counts = jnp.where(positions == emptiest, ANC // 2, counts)
    counts = jnp.where(positions == fullest, ANC, counts)
    return counts.reshape(2, NPAN).astype(jnp.int32)


def with_ends(array, stream_key, smallest, largest):
    longest = array.shape.index(max(array.shape))
    spots = []
    for shift in (0, 1):
        where = [jax.random.randint(jax.random.fold_in(stream_key, axis), (), 0, length) for axis, length in enumerate(array.shape)]
        where[longest] = (where[longest] + shift) % array.shape[longest]
        spots.append(tuple(where))
    return array.at[spots[0]].set(smallest).at[spots[1]].set(largest)


def strengthened(values, rng, source, target, parts, factor):
    owner, partner = [(jnp.arange(values.shape[position]) // (values.shape[position] // parts)).reshape([-1 if axis == position else 1 for axis in range(values.ndim)]) for position in (source, target)]
    chosen = jax.random.permutation(rng, parts)[partner]
    strong = (owner == chosen) | (owner == (partner + parts // 2) % parts)
    return jnp.where(strong, factor * values, values)


def steps_of(stream_key, shape, shards, least, top_value):
    def one(dim, shards_of):
        draws = jax.random.uniform(jax.random.fold_in(jax.random.fold_in(stream_key, 6), dim), (shards_of,), jnp.float32, least / len(shards), top_value / len(shards))
        return jnp.repeat(jnp.exp(draws), shape[dim] // shards_of).reshape((-1,) + (1,) * (len(shape) - dim - 1))

    level = one(*shards[0])
    for cut in shards[1:]:
        level = level * one(*cut)
    return level


def gaussian(rng, dims, scale, reach, shards=(), kind=jnp.bfloat16):
    entries = jax.random.normal(rng, dims, jnp.float32) * scale
    if len(shards) > 0:
        entries = steps_of(rng, dims, shards, -0.22, 0.18) * entries
    return jnp.clip(entries, min=-reach, max=reach).astype(kind)


def heavy_noise(key, dims, scale, bound, shards, heavy, kind=jnp.bfloat16):
    values = scale * jax.random.normal(key, dims, jnp.float32)
    if shards:
        values = values * steps_of(key, dims, shards, -0.22, 0.18)
    return jnp.clip(strengthened(values, jax.random.fold_in(key, 3), *heavy), -bound, bound).astype(kind)


def setup_inputs(seed: int = 0) -> dict:
    streams_of = jax.random.split(jax.random.key(seed), 11)
    return {
        "right_sides": gaussian(streams_of[0], (3, NPAN, PW, RHS), 1.0, 6.0, ((2, 4),), jnp.float32),
        "diag_inverse": draw_diag_inverse(jax.random.fold_in(streams_of[10], 71), 0),
        "sub_blocks": gaussian(streams_of[2], (3, NPAN, NPAN, PW, PW), (NPAN * PW) ** -0.5, 0.125, ((3, 4), (4, 8)), jnp.float32),
        "block_mask": with_ends((jax.random.randint(streams_of[3], (3, NPAN, NPAN), 0, 4) < 3).astype(jnp.int32), jax.random.fold_in(streams_of[3], 1), 0, 1),
        "anc_values": gaussian(streams_of[4], (2, NPAN, ANC, PW), (2 * NPAN * PW) ** -0.5, 0.09375, ((2, 4), (3, 8)), jnp.float32),
        "anc_rows": draw_anc_rows(jax.random.fold_in(streams_of[10], 71), 0),
        "anc_count": draw_anc_count(jax.random.fold_in(streams_of[10], 71), 0),
        "far_factor": heavy_noise(streams_of[7], (NPAN, PW, R_FAR), W ** -0.5, 0.1875, ((1, 8), (2, 4)), (1, 2, 8, 2.0), jnp.float32),
        "far_rhs": gaussian(streams_of[8], (R_FAR, RHS), 1.0, 6.0, ((0, 32),), jnp.float32),
        "far_solution": gaussian(streams_of[9], (R_FAR, RHS), ((R_FAR // W) ** -0.5), 4.0, ((0, 4),), jnp.float32),
    }


FULL_PRECISION = lax.Precision.HIGHEST


def product(left, right):
    return jnp.dot(left, right, precision=FULL_PRECISION, preferred_element_type=jnp.float32)


def forward_chain(right_side, inverse, blocks, extra):
    solved = []
    for panel_index in range(NPAN):
        residual = right_side[panel_index] - extra[panel_index]
        for earlier in range(panel_index):
            residual = residual - product(blocks[panel_index, earlier], solved[earlier])
        solved.append(product(inverse[panel_index], residual))
    return jnp.stack(solved)


def backward_chain(forward, inverse, blocks, extra):
    solved = [None] * NPAN
    for panel_index in reversed(range(NPAN)):
        residual = forward[panel_index] - extra[panel_index]
        for later in range(panel_index + 1, NPAN):
            residual = residual - product(blocks[later, panel_index].T, solved[later])
        solved[panel_index] = product(inverse[panel_index].T, residual)
    return jnp.stack(solved)


def reference(right_sides, diag_inverse, sub_blocks, block_mask, anc_values, anc_rows, anc_count, far_factor, far_rhs, far_solution):
    order = jnp.arange(NPAN)
    lower = (order[:, None] > order[None, :]).astype(jnp.float32)
    blocks = sub_blocks * (block_mask.astype(jnp.float32) * lower[None])[:, :, :, None, None]
    zero_extra = jnp.zeros((NPAN, PW, RHS), jnp.float32)
    children = [forward_chain(right_sides[child_index], diag_inverse[child_index], blocks[child_index], zero_extra) for child_index in range(2)]
    live_rows = (jnp.arange(ANC)[None, None, :] < anc_count[:, :, None]).astype(jnp.float32)
    spread = jnp.zeros((NPAN * PW, RHS), jnp.float32)
    for child_index in range(2):
        for panel_index in range(NPAN):
            update = product(anc_values[child_index, panel_index], children[child_index][panel_index])
            update = update * live_rows[child_index, panel_index][:, None]
            spread = spread.at[anc_rows[child_index, panel_index]].add(update)
    parent = forward_chain(right_sides[2], diag_inverse[2], blocks[2], spread.reshape(NPAN, PW, RHS))
    far_update = far_rhs - jnp.einsum("pjr,pjk->rk", far_factor, parent, precision=FULL_PRECISION)
    far_back = jnp.einsum("pjr,rk->pjk", far_factor, far_solution, precision=FULL_PRECISION)
    parent_solution = backward_chain(parent, diag_inverse[2], blocks[2], far_back)
    parent_flat = parent_solution.reshape(NPAN * PW, RHS)
    child_solutions = []
    for child_index in range(2):
        picked = parent_flat[anc_rows[child_index]] * live_rows[child_index][:, :, None]
        extra = jnp.einsum("paj,pak->pjk", anc_values[child_index], picked, precision=FULL_PRECISION)
        child_solutions.append(backward_chain(children[child_index], diag_inverse[child_index], blocks[child_index], extra))
    forward_solution = jnp.stack(children + [parent])
    solution = jnp.stack(child_solutions + [parent_solution])
    return forward_solution, solution, far_update
```

```python
import functools

import jax
import jax.numpy as jnp
from jax import lax
from jax.experimental import pallas as pl
from jax.experimental.pallas import tpu as pltpu
from jax.sharding import PartitionSpec as P

MESH = pl.DeviceIdType.MESH
NN = (((1,), (0,)), ((), ()))
NT = (((1,), (1,)), ((), ()))
VMEM_LIMIT = 56 * 1024 * 1024


def halves(value):
    high = value.astype(jnp.bfloat16)
    low = (value - high.astype(jnp.float32)).astype(jnp.bfloat16)
    return high, low


def product(left, right, dims):
    left_high, left_low = halves(left)
    right_high, right_low = halves(right)
    rows = left.shape[0]
    both = lax.dot_general(
        jnp.concatenate([left_high, left_low], axis=0),
        right_high,
        dims,
        preferred_element_type=jnp.float32,
    )
    cross = lax.dot_general(left_high, right_low, dims, preferred_element_type=jnp.float32)
    return both[:rows] + (both[rows:] + cross)


def selected(left, choice, dims):
    high, low = halves(left)
    least = (left - high.astype(jnp.float32) - low.astype(jnp.float32)).astype(jnp.bfloat16)
    rows = left.shape[0]
    stacked = lax.dot_general(
        jnp.concatenate([high, low, least], axis=0),
        choice,
        dims,
        preferred_element_type=jnp.float32,
    )
    return stacked[:rows] + (stacked[rows : 2 * rows] + stacked[2 * rows :])


def enter(peers, me):
    barrier = pltpu.get_barrier_semaphore()
    for offset in range(1, peers):
        pl.semaphore_signal(
            barrier,
            inc=1,
            device_id={"row": lax.rem(me + offset, peers)},
            device_id_type=MESH,
        )
    pl.semaphore_wait(barrier, peers - 1)


def send_all(source_of, landing, send_sems, recv_sems, step, peers, me):
    copies = []
    for offset in range(1, peers):
        dest = lax.rem(me + offset, peers)
        copy = pltpu.make_async_remote_copy(
            src_ref=source_of(dest),
            dst_ref=landing,
            send_sem=send_sems.at[step, offset],
            recv_sem=recv_sems.at[step, offset],
            device_id={"row": dest},
            device_id_type=MESH,
        )
        copy.start()
        copies.append(copy)
    return copies


def pair_table(panels):
    pairs = [(later, earlier) for later in range(panels) for earlier in range(later)]
    return {pair: index for index, pair in enumerate(pairs)}, pairs


def tile_of(ref, index, lanes):
    value = ref[:, index, :, 0:lanes]
    return value.reshape(value.shape[0] * value.shape[1], lanes)


def forward_kernel(
    peers,
    panels,
    right_ref,
    inverse_ref,
    child_ref,
    parent_ref,
    choice_ref,
    slices_ref,
    whole_ref,
    gathered,
    parts,
    arrived,
    send_sems,
    recv_sems,
):
    me = lax.axis_index("row")
    pair_of, pairs = pair_table(panels)
    count = len(pairs)
    rows = right_ref.shape[3]
    enter(peers, me)
    started = []

    def spread(step, separators):
        copies = send_all(
            lambda dest: gathered.at[step, me, pl.ds(0, separators)],
            gathered.at[step, me, pl.ds(0, separators)],
            send_sems,
            recv_sems,
            step,
            peers,
            me,
        )
        for copy in copies:
            copy.wait_recv()
        started.extend(copies)
        return [
            jnp.concatenate([gathered[step, peer, index] for peer in range(peers)], axis=1)
            for index in range(separators)
        ]

    solved = [[], []]
    for panel in range(panels):
        for child in range(2):
            residual = right_ref[child, panel]
            for earlier in range(panel):
                tile = tile_of(child_ref, child * count + pair_of[panel, earlier], rows)
                residual = residual - product(solved[child][earlier], tile, NN)
            gathered[panel, me, child] = residual
        whole = spread(panel, 2)
        for child in range(2):
            value = product(whole[child], inverse_ref[child, panel], NT)
            solved[child].append(value)
            for peer in range(peers):
                parts[peer, :, 0:rows] = value[:, peer * rows : (peer + 1) * rows]
            slices_ref[child, panel] = parts[me, :, 0:rows]
    updates = []
    for child in range(2):
        for panel in range(panels):
            tile = tile_of(child_ref, 2 * count + child * panels + panel, child_ref.shape[3])
            updates.append(product(solved[child][panel], tile, NN))
    update = selected(jnp.concatenate(updates, axis=1), choice_ref[...], NN)
    width = peers * rows
    for peer in range(peers):
        for panel in range(panels):
            begin = panel * width + peer * rows
            parts[peer, :, panel * rows : (panel + 1) * rows] = update[:, begin : begin + rows]
    step = 2 * panels
    copies = send_all(
        lambda dest: parts.at[dest], arrived.at[me], send_sems, recv_sems, step, peers, me
    )
    for copy in copies:
        copy.wait_recv()
    started.extend(copies)
    ancestor = parts[me]
    for offset in range(1, peers):
        ancestor = ancestor + arrived[lax.rem(me + offset, peers)]
    solved = []
    for panel in range(panels):
        residual = right_ref[2, panel] - ancestor[:, panel * rows : (panel + 1) * rows]
        for earlier in range(panel):
            tile = tile_of(parent_ref, pair_of[panel, earlier], rows)
            residual = residual - product(solved[earlier], tile, NN)
        gathered[panels + panel, me, 0] = residual
        whole = spread(panels + panel, 1)
        value = product(whole[0], inverse_ref[2, panel], NT)
        solved.append(value)
        whole_ref[panel] = value
    for copy in started:
        copy.wait_send()
    for panel in range(panels):
        for peer in range(peers):
            parts[peer, :, 0:rows] = solved[panel][:, peer * rows : (peer + 1) * rows]
        slices_ref[2, panel] = parts[me, :, 0:rows]


def backward_kernel(
    peers,
    panels,
    forward_ref,
    inverse_ref,
    child_ref,
    parent_ref,
    choice_ref,
    far_ref,
    slices_ref,
    gathered,
    parts,
    arrived,
    mine,
    send_sems,
    recv_sems,
):
    me = lax.axis_index("row")
    pair_of, pairs = pair_table(panels)
    count = len(pairs)
    rows = forward_ref.shape[3]
    enter(peers, me)
    started = []

    def summed(step, forward, partials):
        separators = len(partials)
        for index in range(separators):
            for peer in range(peers):
                parts[step, peer, index] = partials[index][:, peer * rows : (peer + 1) * rows]
        copies = send_all(
            lambda dest: parts.at[step, dest, pl.ds(0, separators)],
            arrived.at[step, me, pl.ds(0, separators)],
            send_sems,
            recv_sems,
            2 * step,
            peers,
            me,
        )
        for copy in copies:
            copy.wait_recv()
        started.extend(copies)
        for index in range(separators):
            total = parts[step, me, index]
            for offset in range(1, peers):
                total = total + arrived[step, lax.rem(me + offset, peers), index]
            gathered[step, me, index] = forward[index] - total
        copies = send_all(
            lambda dest: gathered.at[step, me, pl.ds(0, separators)],
            gathered.at[step, me, pl.ds(0, separators)],
            send_sems,
            recv_sems,
            2 * step + 1,
            peers,
            me,
        )
        for copy in copies:
            copy.wait_recv()
        started.extend(copies)
        return [
            jnp.concatenate([gathered[step, peer, index] for peer in range(peers)], axis=1)
            for index in range(separators)
        ]

    def my_slice(value):
        for peer in range(peers):
            mine[peer] = value[:, peer * rows : (peer + 1) * rows]
        return mine[me]

    solved = [None] * panels
    own = [None] * panels
    for panel in reversed(range(panels)):
        partial = far_ref[panel]
        for later in range(panel + 1, panels):
            tile = tile_of(parent_ref, pair_of[later, panel], rows)
            partial = partial + product(own[later], tile, NT)
        step = panels - 1 - panel
        whole = summed(step, [forward_ref[2, panel]], [partial])
        solved[panel] = product(whole[0], inverse_ref[2, panel], NN)
        own[panel] = my_slice(solved[panel])
        slices_ref[2, panel] = own[panel]
    picked = selected(jnp.concatenate(solved, axis=1), choice_ref[...], NT)
    slots = choice_ref.shape[0] // (2 * panels)
    own = [[None] * panels, [None] * panels]
    for panel in reversed(range(panels)):
        partials = []
        for child in range(2):
            place = child * panels + panel
            tile = tile_of(child_ref, 2 * count + place, slots)
            partial = product(picked[:, place * slots : (place + 1) * slots], tile, NT)
            for later in range(panel + 1, panels):
                tile = tile_of(child_ref, child * count + pair_of[later, panel], rows)
                partial = partial + product(own[child][later], tile, NT)
            partials.append(partial)
        step = 2 * panels - 1 - panel
        whole = summed(step, [forward_ref[child, panel] for child in range(2)], partials)
        for child in range(2):
            value = product(whole[child], inverse_ref[child, panel], NN)
            own[child][panel] = my_slice(value)
            slices_ref[child, panel] = own[child][panel]
    for copy in started:
        copy.wait_send()


def on_device(
    peers,
    right_sides,
    diag_inverse,
    sub_blocks,
    block_mask,
    anc_values,
    anc_rows,
    anc_count,
    far_factor,
    far_rhs,
    far_solution,
):
    panels = diag_inverse.shape[1]
    width = diag_inverse.shape[2]
    rows = right_sides.shape[2]
    columns = right_sides.shape[3]
    col_width = sub_blocks.shape[4]
    slots = anc_rows.shape[2]
    _, pairs = pair_table(panels)
    vmem = pl.BlockSpec(memory_space=pltpu.VMEM)

    def lower(separator):
        tiles = [
            jnp.where(block_mask[separator, later, earlier] == 1, sub_blocks[separator, later, earlier], 0.0).T
            for later, earlier in pairs
        ]
        return tiles

    anc_tiles = anc_values.transpose(0, 1, 3, 2).reshape(2 * panels, col_width, slots)
    child_tiles = jnp.stack(lower(0) + lower(1))
    parent_tiles = jnp.stack(lower(2))
    if rows < slots:
        child_tiles = jnp.pad(child_tiles, ((0, 0), (0, 0), (0, slots - rows)))
    child_all = lax.all_gather(jnp.concatenate([child_tiles, anc_tiles]), "col")
    parent_all = lax.all_gather(parent_tiles, "col")

    position = lax.axis_index("row") * slots + jnp.arange(slots)
    live = position[None, None, :] < anc_count[:, :, None]
    wanted = jnp.where(live, anc_rows, -1).reshape(-1)
    choice = (wanted[:, None] == jnp.arange(panels * width)[None, :]).astype(jnp.bfloat16)

    far_back = jnp.einsum(
        "rk,pjr->pkj", far_solution, far_factor, precision=lax.Precision.HIGH
    )
    far_all = lax.all_gather(far_back, "col", axis=0)
    far_whole = far_all.transpose(1, 2, 0, 3).reshape(panels, columns, width)

    right_turned = right_sides.transpose(0, 1, 3, 2)
    slices, whole = pl.pallas_call(
        functools.partial(forward_kernel, peers, panels),
        out_shape=(
            jax.ShapeDtypeStruct((3, panels, columns, rows), jnp.float32),
            jax.ShapeDtypeStruct((panels, columns, width), jnp.float32),
        ),
        in_specs=[vmem] * 5,
        out_specs=(vmem, vmem),
        scratch_shapes=[
            pltpu.VMEM((2 * panels, peers, 2, columns, rows), jnp.float32),
            pltpu.VMEM((peers, columns, panels * rows), jnp.float32),
            pltpu.VMEM((peers, columns, panels * rows), jnp.float32),
            pltpu.SemaphoreType.DMA((2 * panels + 1, peers)),
            pltpu.SemaphoreType.DMA((2 * panels + 1, peers)),
        ],
        compiler_params=pltpu.CompilerParams(
            collective_id=0, has_side_effects=True, vmem_limit_bytes=VMEM_LIMIT
        ),
        name="forward",
    )(right_turned, diag_inverse, child_all, parent_all, choice)

    start = lax.axis_index("col") * col_width
    parent_cols = lax.dynamic_slice_in_dim(whole, start, col_width, 2)
    far_update = far_rhs - lax.psum_scatter(
        jnp.einsum("pjr,pkj->rk", far_factor, parent_cols, precision=lax.Precision.HIGH),
        "col",
        scatter_dimension=0,
        tiled=True,
    )

    turned = pl.pallas_call(
        functools.partial(backward_kernel, peers, panels),
        out_shape=jax.ShapeDtypeStruct((3, panels, columns, rows), jnp.float32),
        in_specs=[vmem] * 6,
        out_specs=vmem,
        scratch_shapes=[
            pltpu.VMEM((2 * panels, peers, 2, columns, rows), jnp.float32),
            pltpu.VMEM((2 * panels, peers, 2, columns, rows), jnp.float32),
            pltpu.VMEM((2 * panels, peers, 2, columns, rows), jnp.float32),
            pltpu.VMEM((peers, columns, rows), jnp.float32),
            pltpu.SemaphoreType.DMA((4 * panels, peers)),
            pltpu.SemaphoreType.DMA((4 * panels, peers)),
        ],
        compiler_params=pltpu.CompilerParams(
            collective_id=1, has_side_effects=True, vmem_limit_bytes=VMEM_LIMIT
        ),
        name="backward",
    )(slices, diag_inverse, child_all, parent_all, choice, far_whole)
    return (slices.transpose(0, 1, 3, 2), turned.transpose(0, 1, 3, 2), far_update)


def solution(mesh):
    in_specs = (
        P(None, None, "row", None),
        P(),
        P(None, None, None, "row", "col"),
        P(),
        P(None, None, "row", "col"),
        P(None, None, "row"),
        P(),
        P(None, "col", "row"),
        P(("row", "col"), None),
        P("row", None),
    )
    out_specs = (P(None, None, "row", None), P(None, None, "row", None), P(("row", "col"), None))
    return jax.shard_map(
        functools.partial(on_device, mesh.shape["row"]),
        mesh=mesh,
        in_specs=in_specs,
        out_specs=out_specs,
        check_vma=False,
    )
```

```python
import functools

import jax
import jax.numpy as jnp
from jax import lax
from jax.experimental import pallas as pl
from jax.experimental.pallas import tpu as pltpu
from jax.sharding import PartitionSpec as P

MESH = pl.DeviceIdType.MESH
NN = (((1,), (0,)), ((), ()))
NT = (((1,), (1,)), ((), ()))
VMEM_LIMIT = 56 * 1024 * 1024


def halves(value):
    high = value.astype(jnp.bfloat16)
    low = (value - high.astype(jnp.float32)).astype(jnp.bfloat16)
    return high, low


def product(left, right, dims):
    left_high, left_low = halves(left)
    right_high, right_low = halves(right)
    rows = left.shape[0]
    both = lax.dot_general(
        jnp.concatenate([left_high, left_low], axis=0),
        right_high,
        dims,
        preferred_element_type=jnp.float32,
    )
    cross = lax.dot_general(left_high, right_low, dims, preferred_element_type=jnp.float32)
    return both[:rows] + (both[rows:] + cross)


def selected(left, choice, dims):
    high, low = halves(left)
    least = (left - high.astype(jnp.float32) - low.astype(jnp.float32)).astype(jnp.bfloat16)
    rows = left.shape[0]
    stacked = lax.dot_general(
        jnp.concatenate([high, low, least], axis=0),
        choice,
        dims,
        preferred_element_type=jnp.float32,
    )
    return stacked[:rows] + (stacked[rows : 2 * rows] + stacked[2 * rows :])


LAYERS = 4


def enter(peers, me, group=None):
    barrier = pltpu.get_barrier_semaphore()
    for offset in range(1, peers):
        pl.semaphore_signal(
            barrier,
            inc=1,
            device_id={"row": lax.rem(me + offset, peers)},
            device_id_type=MESH,
        )
    expected = peers - 1
    if group is not None:
        level, lane, lanes = group
        cols = LAYERS * lanes
        for offset in range(1, cols):
            pl.semaphore_signal(
                barrier,
                inc=1,
                device_id={"col": lax.rem(level * lanes + lane + offset, cols)},
                device_id_type=MESH,
            )
        expected = expected + cols - 1
    pl.semaphore_wait(barrier, expected)


def has_level(level):
    return jnp.logical_and(level >= 0, level < LAYERS)


class Relay:
    def __init__(self, tiles, chunks, group, send_sems, recv_sems):
        self.tiles, self.chunks, self.group = tiles, chunks, group
        self.send_sems, self.recv_sems = send_sems, recv_sems
        self.sent = []
        self.time = 0

    def copy(self, chunk, owner, way, dest):
        first, length, _ = self.chunks[chunk]
        part = self.tiles.at[owner, pl.ds(first, length)]
        return pltpu.make_async_remote_copy(
            src_ref=part,
            dst_ref=part,
            send_sem=self.send_sems.at[chunk, owner, way],
            recv_sem=self.recv_sems.at[chunk, owner],
            device_id={"col": dest},
            device_id_type=MESH,
        )

    def along(self, chunk, level, lane, way):
        mine, my_lane, lanes = self.group
        ok = jnp.logical_and(has_level(level), has_level(mine + way))

        def one(wait):
            @pl.when(ok)
            def _():
                copy = self.copy(
                    chunk,
                    level * lanes + lane,
                    0 if way > 0 else 1,
                    (mine + way) * lanes + my_lane,
                )
                copy.wait_send() if wait else copy.start()

        one(False)
        self.sent.append(one)

    def across(self, chunk, level):
        mine, my_lane, lanes = self.group

        def one(wait):
            @pl.when(has_level(level))
            def _():
                for offset in range(1, lanes):
                    copy = self.copy(
                        chunk,
                        level * lanes + my_lane,
                        1 + offset,
                        mine * lanes + lax.rem(my_lane + offset, lanes),
                    )
                    copy.wait_send() if wait else copy.start()

        one(False)
        self.sent.append(one)

    def take(self, chunk, level, lane):
        mine, my_lane, lanes = self.group

        @pl.when(has_level(level))
        def _():
            self.copy(chunk, level * lanes + lane, 0, mine * lanes + my_lane).wait_recv()

    def hop(self, chunk, hop):
        mine, my_lane, lanes = self.group
        lane_first = self.chunks[chunk][2]
        others = [lax.rem(my_lane + offset, lanes) for offset in range(1, lanes)]
        if hop == 0:
            self.across(chunk, mine)
            self.along(chunk, mine, my_lane, 1)
            self.along(chunk, mine, my_lane, -1)
            return
        if lane_first and hop == 1:
            for lane in others:
                self.take(chunk, mine, lane)
                self.along(chunk, mine, lane, 1)
                self.along(chunk, mine, lane, -1)
        if lane_first and hop >= 2:
            for way in (1, -1):
                for lane in others:
                    level = mine - way * (hop - 1)
                    self.take(chunk, level, lane)
                    self.along(chunk, level, lane, way)
        if hop < LAYERS:
            for way in (1, -1):
                level = mine - way * hop
                self.take(chunk, level, my_lane)
                self.along(chunk, level, my_lane, way)
                if not lane_first:
                    self.across(chunk, level)
        if not lane_first and hop == LAYERS:
            for distance in range(1 - LAYERS, LAYERS):
                for lane in others:
                    self.take(chunk, mine + distance, lane)

    def pump(self):
        for chunk in range(len(self.chunks)):
            hop = self.time - chunk
            if 0 <= hop <= LAYERS:
                self.hop(chunk, hop)
        self.time += 1

    def finish(self):
        while self.time < len(self.chunks) + LAYERS:
            self.pump()

    def settle(self):
        for one in self.sent:
            one(True)


def send_all(source_of, landing, send_sems, recv_sems, step, peers, me):
    copies = []
    for offset in range(1, peers):
        dest = lax.rem(me + offset, peers)
        copy = pltpu.make_async_remote_copy(
            src_ref=source_of(dest),
            dst_ref=landing,
            send_sem=send_sems.at[step, offset],
            recv_sem=recv_sems.at[step, offset],
            device_id={"row": dest},
            device_id_type=MESH,
        )
        copy.start()
        copies.append(copy)
    return copies


def pair_table(panels):
    pairs = [(later, earlier) for later in range(panels) for earlier in range(later)]
    return {pair: index for index, pair in enumerate(pairs)}, pairs


def tile_of(ref, index, lanes):
    value = ref[:, index, :, 0:lanes]
    return value.reshape(value.shape[0] * value.shape[1], lanes)


def forward_kernel(
    peers,
    panels,
    right_ref,
    inverse_ref,
    tiles_in,
    choice_ref,
    slices_ref,
    whole_ref,
    tiles_out,
    gathered,
    parts,
    arrived,
    tiles,
    send_sems,
    recv_sems,
    relay_send,
    relay_recv,
    local_sem,
):
    me = lax.axis_index("row")
    lanes = tiles.shape[0] // LAYERS
    column = lax.axis_index("col")
    group = (column // lanes, lax.rem(column, lanes), lanes)
    pair_of, pairs = pair_table(panels)
    count = len(pairs)
    rows = right_ref.shape[3]
    children, parents, ancestors = 0, 2 * count + 2 * panels, 2 * count
    half = panels - 1
    chunks = [
        (0, 2 * (count - half), False),
        (2 * (count - half), 2 * half, True),
        (ancestors, panels, False),
        (ancestors + panels, panels, True),
        (parents, count, False),
        (parents + count, tiles.shape[1] - parents - count, False),
    ]
    tiles[column] = tiles_in[...]
    enter(peers, me, group)
    started = []
    relay = Relay(tiles, chunks, group, relay_send, relay_recv)
    relay.pump()
    relay.pump()

    def spread(step, separators):
        copies = send_all(
            lambda dest: gathered.at[step, me, pl.ds(0, separators)],
            gathered.at[step, me, pl.ds(0, separators)],
            send_sems,
            recv_sems,
            step,
            peers,
            me,
        )
        if relay.time < len(chunks) + LAYERS:
            relay.pump()
        for copy in copies:
            copy.wait_recv()
        started.extend(copies)
        return [
            jnp.concatenate([gathered[step, peer, index] for peer in range(peers)], axis=1)
            for index in range(separators)
        ]

    solved = [[], []]
    for panel in range(panels):
        for child in range(2):
            residual = right_ref[child, panel]
            for earlier in range(panel):
                tile = tile_of(tiles, 2 * pair_of[panel, earlier] + child, rows)
                residual = residual - product(solved[child][earlier], tile, NN)
            gathered[panel, me, child] = residual
        whole = spread(panel, 2)
        for child in range(2):
            value = product(whole[child], inverse_ref[child, panel], NT)
            solved[child].append(value)
            for peer in range(peers):
                parts[peer, :, 0:rows] = value[:, peer * rows : (peer + 1) * rows]
            slices_ref[child, panel] = parts[me, :, 0:rows]
        if panel == 0:
            relay.pump()
            relay.pump()
    updates = []
    for child in range(2):
        for panel in range(panels):
            tile = tile_of(tiles, ancestors + 2 * panel + child, tiles.shape[3])
            updates.append(product(solved[child][panel], tile, NN))
    update = selected(jnp.concatenate(updates, axis=1), choice_ref[...], NN)
    width = peers * rows
    for peer in range(peers):
        for panel in range(panels):
            begin = panel * width + peer * rows
            parts[peer, :, panel * rows : (panel + 1) * rows] = update[:, begin : begin + rows]
    step = 2 * panels
    copies = send_all(
        lambda dest: parts.at[dest], arrived.at[me], send_sems, recv_sems, step, peers, me
    )
    relay.pump()
    for copy in copies:
        copy.wait_recv()
    started.extend(copies)
    ancestor = parts[me]
    for offset in range(1, peers):
        ancestor = ancestor + arrived[lax.rem(me + offset, peers)]
    solved = []
    for panel in range(panels):
        residual = right_ref[2, panel] - ancestor[:, panel * rows : (panel + 1) * rows]
        for earlier in range(panel):
            tile = tile_of(tiles, parents + pair_of[panel, earlier], rows)
            residual = residual - product(solved[earlier], tile, NN)
        gathered[panels + panel, me, 0] = residual
        whole = spread(panels + panel, 1)
        value = product(whole[0], inverse_ref[2, panel], NT)
        solved.append(value)
        whole_ref[panel] = value
    relay.finish()
    keep = pltpu.make_async_copy(tiles, tiles_out, local_sem)
    keep.start()
    for copy in started:
        copy.wait_send()
    relay.settle()
    for panel in range(panels):
        for peer in range(peers):
            parts[peer, :, 0:rows] = solved[panel][:, peer * rows : (peer + 1) * rows]
        slices_ref[2, panel] = parts[me, :, 0:rows]
    keep.wait()


def backward_kernel(
    peers,
    panels,
    forward_ref,
    inverse_ref,
    tiles_ref,
    choice_ref,
    slices_ref,
    gathered,
    parts,
    arrived,
    mine,
    send_sems,
    recv_sems,
):
    me = lax.axis_index("row")
    pair_of, pairs = pair_table(panels)
    count = len(pairs)
    rows = forward_ref.shape[3]
    parents, ancestors = 2 * count + 2 * panels, 2 * count
    columns = forward_ref.shape[2]
    enter(peers, me)
    started = []
    far_parts = []
    for index in range(parents + count, tiles_ref.shape[1]):
        turned = tile_of(tiles_ref, index, tiles_ref.shape[3]).T
        for begin in range(0, turned.shape[0], columns):
            far_parts.append(turned[begin : begin + columns])

    def summed(step, forward, partials):
        separators = len(partials)
        for index in range(separators):
            for peer in range(peers):
                parts[step, peer, index] = partials[index][:, peer * rows : (peer + 1) * rows]
        copies = send_all(
            lambda dest: parts.at[step, dest, pl.ds(0, separators)],
            arrived.at[step, me, pl.ds(0, separators)],
            send_sems,
            recv_sems,
            2 * step,
            peers,
            me,
        )
        for copy in copies:
            copy.wait_recv()
        started.extend(copies)
        for index in range(separators):
            total = parts[step, me, index]
            for offset in range(1, peers):
                total = total + arrived[step, lax.rem(me + offset, peers), index]
            gathered[step, me, index] = forward[index] - total
        copies = send_all(
            lambda dest: gathered.at[step, me, pl.ds(0, separators)],
            gathered.at[step, me, pl.ds(0, separators)],
            send_sems,
            recv_sems,
            2 * step + 1,
            peers,
            me,
        )
        for copy in copies:
            copy.wait_recv()
        started.extend(copies)
        return [
            jnp.concatenate([gathered[step, peer, index] for peer in range(peers)], axis=1)
            for index in range(separators)
        ]

    def my_slice(value):
        for peer in range(peers):
            mine[peer] = value[:, peer * rows : (peer + 1) * rows]
        return mine[me]

    solved = [None] * panels
    own = [None] * panels
    for panel in reversed(range(panels)):
        partial = far_parts[panel]
        for later in range(panel + 1, panels):
            tile = tile_of(tiles_ref, parents + pair_of[later, panel], rows)
            partial = partial + product(own[later], tile, NT)
        step = panels - 1 - panel
        whole = summed(step, [forward_ref[2, panel]], [partial])
        solved[panel] = product(whole[0], inverse_ref[2, panel], NN)
        own[panel] = my_slice(solved[panel])
        slices_ref[2, panel] = own[panel]
    picked = selected(jnp.concatenate(solved, axis=1), choice_ref[...], NT)
    slots = choice_ref.shape[0] // (2 * panels)
    own = [[None] * panels, [None] * panels]
    for panel in reversed(range(panels)):
        partials = []
        for child in range(2):
            place = child * panels + panel
            tile = tile_of(tiles_ref, ancestors + 2 * panel + child, slots)
            partial = product(picked[:, place * slots : (place + 1) * slots], tile, NT)
            for later in range(panel + 1, panels):
                tile = tile_of(tiles_ref, 2 * pair_of[later, panel] + child, rows)
                partial = partial + product(own[child][later], tile, NT)
            partials.append(partial)
        step = 2 * panels - 1 - panel
        whole = summed(step, [forward_ref[child, panel] for child in range(2)], partials)
        for child in range(2):
            value = product(whole[child], inverse_ref[child, panel], NN)
            own[child][panel] = my_slice(value)
            slices_ref[child, panel] = own[child][panel]
    for copy in started:
        copy.wait_send()


def on_device(
    peers,
    right_sides,
    diag_inverse,
    sub_blocks,
    block_mask,
    anc_values,
    anc_rows,
    anc_count,
    far_factor,
    far_rhs,
    far_solution,
):
    panels = diag_inverse.shape[1]
    width = diag_inverse.shape[2]
    rows = right_sides.shape[2]
    columns = right_sides.shape[3]
    col_width = sub_blocks.shape[4]
    slots = anc_rows.shape[2]
    _, pairs = pair_table(panels)
    vmem = pl.BlockSpec(memory_space=pltpu.VMEM)

    def lower(separator):
        tiles = [
            jnp.where(block_mask[separator, later, earlier] == 1, sub_blocks[separator, later, earlier], 0.0).T
            for later, earlier in pairs
        ]
        return tiles

    anc_tiles = anc_values.transpose(1, 0, 3, 2).reshape(2 * panels, col_width, slots)
    children = [tile for pair in zip(lower(0), lower(1)) for tile in pair]
    block_tiles = [jnp.stack(children), jnp.stack(lower(2))]
    if rows < slots:
        block_tiles = [
            jnp.pad(tiles, ((0, 0), (0, 0), (0, slots - rows))) for tiles in block_tiles
        ]
    beside = slots // columns
    far_back = jnp.einsum(
        "pjr,rk->pjk", far_factor, far_solution, precision=lax.Precision.HIGH
    )
    far_tiles = (
        far_back.reshape(panels // beside, beside, col_width, columns)
        .transpose(0, 2, 1, 3)
        .reshape(panels // beside, col_width, slots)
    )
    tiles = jnp.concatenate([block_tiles[0], anc_tiles, block_tiles[1], far_tiles])
    cols = width // col_width

    position = lax.axis_index("row") * slots + jnp.arange(slots)
    live = position[None, None, :] < anc_count[:, :, None]
    wanted = jnp.where(live, anc_rows, -1).reshape(-1)
    choice = (wanted[:, None] == jnp.arange(panels * width)[None, :]).astype(jnp.bfloat16)

    right_turned = right_sides.transpose(0, 1, 3, 2)
    slices, whole, tiles_all = pl.pallas_call(
        functools.partial(forward_kernel, peers, panels),
        out_shape=(
            jax.ShapeDtypeStruct((3, panels, columns, rows), jnp.float32),
            jax.ShapeDtypeStruct((panels, columns, width), jnp.float32),
            jax.ShapeDtypeStruct((cols,) + tiles.shape, jnp.float32),
        ),
        in_specs=[vmem] * 4,
        out_specs=(vmem, vmem, pl.BlockSpec(memory_space=pl.ANY)),
        scratch_shapes=[
            pltpu.VMEM((2 * panels, peers, 2, columns, rows), jnp.float32),
            pltpu.VMEM((peers, columns, panels * rows), jnp.float32),
            pltpu.VMEM((peers, columns, panels * rows), jnp.float32),
            pltpu.VMEM((cols,) + tiles.shape, jnp.float32),
            pltpu.SemaphoreType.DMA((2 * panels + 1, peers)),
            pltpu.SemaphoreType.DMA((2 * panels + 1, peers)),
            pltpu.SemaphoreType.DMA((6, cols, 1 + cols // LAYERS)),
            pltpu.SemaphoreType.DMA((6, cols)),
            pltpu.SemaphoreType.DMA,
        ],
        compiler_params=pltpu.CompilerParams(
            collective_id=0, has_side_effects=True, vmem_limit_bytes=VMEM_LIMIT
        ),
        name="forward",
    )(right_turned, diag_inverse, tiles, choice)

    start = lax.axis_index("col") * col_width
    parent_cols = lax.dynamic_slice_in_dim(whole, start, col_width, 2)
    far_update = far_rhs - lax.psum_scatter(
        jnp.einsum("pjr,pkj->rk", far_factor, parent_cols, precision=lax.Precision.HIGH),
        "col",
        scatter_dimension=0,
        tiled=True,
    )

    turned = pl.pallas_call(
        functools.partial(backward_kernel, peers, panels),
        out_shape=jax.ShapeDtypeStruct((3, panels, columns, rows), jnp.float32),
        in_specs=[vmem] * 4,
        out_specs=vmem,
        scratch_shapes=[
            pltpu.VMEM((2 * panels, peers, 2, columns, rows), jnp.float32),
            pltpu.VMEM((2 * panels, peers, 2, columns, rows), jnp.float32),
            pltpu.VMEM((2 * panels, peers, 2, columns, rows), jnp.float32),
            pltpu.VMEM((peers, columns, rows), jnp.float32),
            pltpu.SemaphoreType.DMA((4 * panels, peers)),
            pltpu.SemaphoreType.DMA((4 * panels, peers)),
        ],
        compiler_params=pltpu.CompilerParams(
            collective_id=1, has_side_effects=True, vmem_limit_bytes=VMEM_LIMIT
        ),
        name="backward",
    )(slices, diag_inverse, tiles_all, choice)
    return (slices.transpose(0, 1, 3, 2), turned.transpose(0, 1, 3, 2), far_update)


def solution(mesh):
    in_specs = (
        P(None, None, "row", None),
        P(),
        P(None, None, None, "row", "col"),
        P(),
        P(None, None, "row", "col"),
        P(None, None, "row"),
        P(),
        P(None, "col", "row"),
        P(("row", "col"), None),
        P("row", None),
    )
    out_specs = (P(None, None, "row", None), P(None, None, "row", None), P(("row", "col"), None))
    return jax.shard_map(
        functools.partial(on_device, mesh.shape["row"]),
        mesh=mesh,
        in_specs=in_specs,
        out_specs=out_specs,
        check_vma=False,
    )
```

```python
import functools

import jax
import jax.numpy as jnp
from jax import lax
from jax.experimental import pallas as pl
from jax.experimental.pallas import tpu as pltpu
from jax.sharding import PartitionSpec as P

MESH = pl.DeviceIdType.MESH
NN = (((1,), (0,)), ((), ()))
NT = (((1,), (1,)), ((), ()))
VMEM_LIMIT = 56 * 1024 * 1024


def halves(value):
    high = value.astype(jnp.bfloat16)
    low = (value - high.astype(jnp.float32)).astype(jnp.bfloat16)
    return high, low


def split_product(left, right, dims):
    rows = left[0].shape[0]
    both = lax.dot_general(
        jnp.concatenate(left, axis=0), right[0], dims, preferred_element_type=jnp.float32
    )
    cross = lax.dot_general(left[0], right[1], dims, preferred_element_type=jnp.float32)
    return both[:rows] + (both[rows:] + cross)


def product(left, right, dims):
    return split_product(halves(left), halves(right), dims)


def selected(left, choice, dims):
    high, low = halves(left)
    least = (left - high.astype(jnp.float32) - low.astype(jnp.float32)).astype(jnp.bfloat16)
    rows = left.shape[0]
    stacked = lax.dot_general(
        jnp.concatenate([high, low, least], axis=0),
        choice,
        dims,
        preferred_element_type=jnp.float32,
    )
    return stacked[:rows] + (stacked[rows : 2 * rows] + stacked[2 * rows :])


LAYERS = 4


def enter(peers, me, group=None):
    barrier = pltpu.get_barrier_semaphore()
    for offset in range(1, peers):
        pl.semaphore_signal(
            barrier,
            inc=1,
            device_id={"row": lax.rem(me + offset, peers)},
            device_id_type=MESH,
        )
    expected = peers - 1
    if group is not None:
        level, lane, lanes = group
        cols = LAYERS * lanes
        for offset in range(1, cols):
            pl.semaphore_signal(
                barrier,
                inc=1,
                device_id={"col": lax.rem(level * lanes + lane + offset, cols)},
                device_id_type=MESH,
            )
        expected = expected + cols - 1
    pl.semaphore_wait(barrier, expected)


def has_level(level):
    return jnp.logical_and(level >= 0, level < LAYERS)


class Relay:
    def __init__(self, tiles, chunks, group, send_sems, recv_sems):
        self.tiles, self.chunks, self.group = tiles, chunks, group
        self.send_sems, self.recv_sems = send_sems, recv_sems
        self.sent = []
        self.time = 0

    def copy(self, chunk, owner, way, dest):
        first, length, _ = self.chunks[chunk]
        part = self.tiles.at[owner, pl.ds(first, length)]
        return pltpu.make_async_remote_copy(
            src_ref=part,
            dst_ref=part,
            send_sem=self.send_sems.at[chunk, owner, way],
            recv_sem=self.recv_sems.at[chunk, owner],
            device_id={"col": dest},
            device_id_type=MESH,
        )

    def along(self, chunk, level, lane, way):
        mine, my_lane, lanes = self.group
        ok = jnp.logical_and(has_level(level), has_level(mine + way))

        def one(wait):
            @pl.when(ok)
            def _():
                copy = self.copy(
                    chunk,
                    level * lanes + lane,
                    0 if way > 0 else 1,
                    (mine + way) * lanes + my_lane,
                )
                copy.wait_send() if wait else copy.start()

        one(False)
        self.sent.append(one)

    def across(self, chunk, level):
        mine, my_lane, lanes = self.group

        def one(wait):
            @pl.when(has_level(level))
            def _():
                for offset in range(1, lanes):
                    copy = self.copy(
                        chunk,
                        level * lanes + my_lane,
                        1 + offset,
                        mine * lanes + lax.rem(my_lane + offset, lanes),
                    )
                    copy.wait_send() if wait else copy.start()

        one(False)
        self.sent.append(one)

    def take(self, chunk, level, lane):
        mine, my_lane, lanes = self.group

        @pl.when(has_level(level))
        def _():
            self.copy(chunk, level * lanes + lane, 0, mine * lanes + my_lane).wait_recv()

    def hop(self, chunk, hop):
        mine, my_lane, lanes = self.group
        lane_first = self.chunks[chunk][2]
        others = [lax.rem(my_lane + offset, lanes) for offset in range(1, lanes)]
        if hop == 0:
            self.across(chunk, mine)
            self.along(chunk, mine, my_lane, 1)
            self.along(chunk, mine, my_lane, -1)
            return
        if lane_first and hop == 1:
            for lane in others:
                self.take(chunk, mine, lane)
                self.along(chunk, mine, lane, 1)
                self.along(chunk, mine, lane, -1)
        if lane_first and hop >= 2:
            for way in (1, -1):
                for lane in others:
                    level = mine - way * (hop - 1)
                    self.take(chunk, level, lane)
                    self.along(chunk, level, lane, way)
        if hop < LAYERS:
            for way in (1, -1):
                level = mine - way * hop
                self.take(chunk, level, my_lane)
                self.along(chunk, level, my_lane, way)
                if not lane_first:
                    self.across(chunk, level)
        if not lane_first and hop == LAYERS:
            for distance in range(1 - LAYERS, LAYERS):
                for lane in others:
                    self.take(chunk, mine + distance, lane)

    def pump(self):
        for chunk in range(len(self.chunks)):
            hop = self.time - chunk
            if 0 <= hop <= LAYERS:
                self.hop(chunk, hop)
        self.time += 1

    def finish(self):
        while self.time < len(self.chunks) + LAYERS:
            self.pump()

    def settle(self):
        for one in self.sent:
            one(True)


def send_all(source_of, landing, send_sems, recv_sems, step, peers, me):
    copies = []
    for offset in range(1, peers):
        dest = lax.rem(me + offset, peers)
        copy = pltpu.make_async_remote_copy(
            src_ref=source_of(dest),
            dst_ref=landing,
            send_sem=send_sems.at[step, offset],
            recv_sem=recv_sems.at[step, offset],
            device_id={"row": dest},
            device_id_type=MESH,
        )
        copy.start()
        copies.append(copy)
    return copies


def pair_table(panels):
    pairs = [(later, earlier) for later in range(panels) for earlier in range(later)]
    return {pair: index for index, pair in enumerate(pairs)}, pairs


def tile_of(ref, index, lanes):
    value = ref[:, index, :, 0:lanes]
    return value.reshape(value.shape[0] * value.shape[1], lanes)


def forward_kernel(
    peers,
    panels,
    right_ref,
    inverse_ref,
    mask_ref,
    block_ref,
    anc_ref,
    far_ref,
    choice_ref,
    slices_ref,
    whole_ref,
    tiles_out,
    gathered,
    parts,
    arrived,
    tiles,
    send_sems,
    recv_sems,
    relay_send,
    relay_recv,
    local_sem,
):
    me = lax.axis_index("row")
    lanes = tiles.shape[0] // LAYERS
    column = lax.axis_index("col")
    group = (column // lanes, lax.rem(column, lanes), lanes)
    pair_of, pairs = pair_table(panels)
    count = len(pairs)
    rows = right_ref.shape[3]
    children, parents, ancestors = 0, 2 * count + 2 * panels, 2 * count
    half = panels - 1
    chunks = [
        (0, 2 * (count - half), False),
        (2 * (count - half), 2 * half, False),
        (ancestors, panels, False),
        (ancestors + panels, panels, False),
        (parents, count, False),
        (parents + count, tiles.shape[1] - parents - count, False),
    ]
    beyond = tiles.shape[3] - rows

    def place(index, separator, later, earlier):
        tile = block_ref[separator, later, earlier]
        tile = jnp.where(mask_ref[separator, later, earlier] == 1, tile, 0.0)
        if beyond:
            tile = jnp.concatenate([tile, jnp.zeros((tile.shape[0], beyond), tile.dtype)], axis=1)
        tiles[column, index] = tile

    for index, (later, earlier) in enumerate(pairs):
        place(2 * index, 0, later, earlier)
        place(2 * index + 1, 1, later, earlier)
        place(parents + index, 2, later, earlier)
    for panel in range(panels):
        for child in range(2):
            tiles[column, ancestors + 2 * panel + child] = anc_ref[child, panel]
    for index in range(far_ref.shape[0]):
        tiles[column, parents + count + index] = far_ref[index]
    enter(peers, me, group)
    started = []
    relay = Relay(tiles, chunks, group, relay_send, relay_recv)
    relay.pump()
    relay.pump()

    def spread(step, separators, meanwhile):
        copies = send_all(
            lambda dest: gathered.at[step, me, pl.ds(0, separators)],
            gathered.at[step, me, pl.ds(0, separators)],
            send_sems,
            recv_sems,
            step,
            peers,
            me,
        )
        if relay.time < len(chunks) + LAYERS:
            relay.pump()
        ready = meanwhile()
        for copy in copies:
            copy.wait_recv()
        started.extend(copies)
        whole = [
            jnp.concatenate([gathered[step, peer, index] for peer in range(peers)], axis=1)
            for index in range(separators)
        ]
        return whole, ready

    solved = [[], []]
    pending = [right_ref[child, 0] for child in range(2)]
    for panel in range(panels):
        for child in range(2):
            gathered[panel, me, child] = pending[child]

        def ahead():
            inverses = [halves(inverse_ref[child, panel]) for child in range(2)]
            rest = [None, None]
            if panel + 1 < panels:
                for child in range(2):
                    rest[child] = right_ref[child, panel + 1]
                    for earlier in range(panel):
                        tile = tile_of(tiles, 2 * pair_of[panel + 1, earlier] + child, rows)
                        rest[child] = rest[child] - product(solved[child][earlier], tile, NN)
            return inverses, rest

        whole, (inverses, pending) = spread(panel, 2, ahead)
        for child in range(2):
            value = split_product(halves(whole[child]), inverses[child], NT)
            solved[child].append(value)
            for peer in range(peers):
                parts[peer, :, 0:rows] = value[:, peer * rows : (peer + 1) * rows]
            slices_ref[child, panel] = parts[me, :, 0:rows]
        if panel == 0:
            relay.pump()
            relay.pump()
        if panel + 1 < panels:
            for child in range(2):
                tile = tile_of(tiles, 2 * pair_of[panel + 1, panel] + child, rows)
                pending[child] = pending[child] - product(solved[child][panel], tile, NN)
    updates = []
    for child in range(2):
        for panel in range(panels):
            tile = tile_of(tiles, ancestors + 2 * panel + child, tiles.shape[3])
            updates.append(product(solved[child][panel], tile, NN))
    update = selected(jnp.concatenate(updates, axis=1), choice_ref[...], NN)
    width = peers * rows
    for peer in range(peers):
        for panel in range(panels):
            begin = panel * width + peer * rows
            parts[peer, :, panel * rows : (panel + 1) * rows] = update[:, begin : begin + rows]
    step = 2 * panels
    copies = send_all(
        lambda dest: parts.at[dest], arrived.at[me], send_sems, recv_sems, step, peers, me
    )
    relay.pump()
    for copy in copies:
        copy.wait_recv()
    started.extend(copies)
    ancestor = parts[me]
    for offset in range(1, peers):
        ancestor = ancestor + arrived[lax.rem(me + offset, peers)]
    solved = []
    parent_right = [
        right_ref[2, panel] - ancestor[:, panel * rows : (panel + 1) * rows]
        for panel in range(panels)
    ]
    pending = parent_right[0]
    for panel in range(panels):
        gathered[panels + panel, me, 0] = pending

        def ahead():
            rest = None
            if panel + 1 < panels:
                rest = parent_right[panel + 1]
                for earlier in range(panel):
                    tile = tile_of(tiles, parents + pair_of[panel + 1, earlier], rows)
                    rest = rest - product(solved[earlier], tile, NN)
            return halves(inverse_ref[2, panel]), rest

        whole, (inverse, pending) = spread(panels + panel, 1, ahead)
        value = split_product(halves(whole[0]), inverse, NT)
        solved.append(value)
        whole_ref[panel] = value
        if panel + 1 < panels:
            tile = tile_of(tiles, parents + pair_of[panel + 1, panel], rows)
            pending = pending - product(value, tile, NN)
    relay.finish()
    keep = pltpu.make_async_copy(tiles, tiles_out, local_sem)
    keep.start()
    for copy in started:
        copy.wait_send()
    relay.settle()
    for panel in range(panels):
        for peer in range(peers):
            parts[peer, :, 0:rows] = solved[panel][:, peer * rows : (peer + 1) * rows]
        slices_ref[2, panel] = parts[me, :, 0:rows]
    keep.wait()


def backward_kernel(
    peers,
    panels,
    forward_ref,
    inverse_ref,
    tiles_ref,
    choice_ref,
    slices_ref,
    gathered,
    parts,
    arrived,
    mine,
    send_sems,
    recv_sems,
):
    me = lax.axis_index("row")
    pair_of, pairs = pair_table(panels)
    count = len(pairs)
    rows = forward_ref.shape[3]
    parents, ancestors = 2 * count + 2 * panels, 2 * count
    columns = forward_ref.shape[2]
    enter(peers, me)
    started = []
    far_parts = []
    for index in range(parents + count, tiles_ref.shape[1]):
        turned = tile_of(tiles_ref, index, tiles_ref.shape[3]).T
        for begin in range(0, turned.shape[0], columns):
            far_parts.append(turned[begin : begin + columns])

    def summed(step, forward, partials, first, second):
        separators = len(partials)
        for index in range(separators):
            for peer in range(peers):
                parts[step, peer, index] = partials[index][:, peer * rows : (peer + 1) * rows]
        copies = send_all(
            lambda dest: parts.at[step, dest, pl.ds(0, separators)],
            arrived.at[step, me, pl.ds(0, separators)],
            send_sems,
            recv_sems,
            2 * step,
            peers,
            me,
        )
        early = first()
        for copy in copies:
            copy.wait_recv()
        started.extend(copies)
        for index in range(separators):
            total = parts[step, me, index]
            for offset in range(1, peers):
                total = total + arrived[step, lax.rem(me + offset, peers), index]
            gathered[step, me, index] = forward[index] - total
        copies = send_all(
            lambda dest: gathered.at[step, me, pl.ds(0, separators)],
            gathered.at[step, me, pl.ds(0, separators)],
            send_sems,
            recv_sems,
            2 * step + 1,
            peers,
            me,
        )
        late = second()
        for copy in copies:
            copy.wait_recv()
        started.extend(copies)
        whole = [
            jnp.concatenate([gathered[step, peer, index] for peer in range(peers)], axis=1)
            for index in range(separators)
        ]
        return whole, early, late

    def my_slice(value):
        for peer in range(peers):
            mine[peer] = value[:, peer * rows : (peer + 1) * rows]
        return mine[me]

    solved = [None] * panels
    own = [None] * panels
    slots = choice_ref.shape[0] // (2 * panels)
    width = peers * rows
    pending = far_parts[panels - 1]
    picked = None
    for panel in reversed(range(panels)):

        def first():
            return halves(inverse_ref[2, panel])

        def second():
            rest, pick = None, picked
            if panel > 0:
                rest = far_parts[panel - 1]
                for later in range(panel + 1, panels):
                    tile = tile_of(tiles_ref, parents + pair_of[later, panel - 1], rows)
                    rest = rest + product(own[later], tile, NT)
            if panel + 1 < panels:
                pick = pick_from(panel + 1, pick)
            return rest, pick

        def pick_from(source, pick):
            chosen = choice_ref[:, source * width : (source + 1) * width]
            more = selected(solved[source], chosen, NT)
            return more if pick is None else pick + more

        step = panels - 1 - panel
        whole, inverse, (rest, picked) = summed(
            step, [forward_ref[2, panel]], [pending], first, second
        )
        solved[panel] = split_product(halves(whole[0]), inverse, NN)
        own[panel] = my_slice(solved[panel])
        slices_ref[2, panel] = own[panel]
        if panel > 0:
            tile = tile_of(tiles_ref, parents + pair_of[panel, panel - 1], rows)
            pending = rest + product(own[panel], tile, NT)
    picked = pick_from(0, picked)

    def from_parent(child, panel):
        place = child * panels + panel
        tile = tile_of(tiles_ref, ancestors + 2 * panel + child, slots)
        return product(picked[:, place * slots : (place + 1) * slots], tile, NT)

    own = [[None] * panels, [None] * panels]
    pending = [from_parent(child, panels - 1) for child in range(2)]
    for panel in reversed(range(panels)):

        def first():
            return [halves(inverse_ref[child, panel]) for child in range(2)]

        def second():
            rest = [None, None]
            if panel > 0:
                for child in range(2):
                    rest[child] = from_parent(child, panel - 1)
                    for later in range(panel + 1, panels):
                        tile = tile_of(tiles_ref, 2 * pair_of[later, panel - 1] + child, rows)
                        rest[child] = rest[child] + product(own[child][later], tile, NT)
            return rest

        step = 2 * panels - 1 - panel
        whole, inverses, rest = summed(
            step, [forward_ref[child, panel] for child in range(2)], pending, first, second
        )
        for child in range(2):
            value = split_product(halves(whole[child]), inverses[child], NN)
            own[child][panel] = my_slice(value)
            slices_ref[child, panel] = own[child][panel]
        if panel > 0:
            for child in range(2):
                tile = tile_of(tiles_ref, 2 * pair_of[panel, panel - 1] + child, rows)
                pending[child] = rest[child] + product(own[child][panel], tile, NT)
    for copy in started:
        copy.wait_send()


def on_device(
    peers,
    right_sides,
    diag_inverse,
    sub_blocks,
    block_mask,
    anc_values,
    anc_rows,
    anc_count,
    far_factor,
    far_rhs,
    far_solution,
):
    panels = diag_inverse.shape[1]
    width = diag_inverse.shape[2]
    rows = right_sides.shape[2]
    columns = right_sides.shape[3]
    col_width = sub_blocks.shape[4]
    slots = anc_rows.shape[2]
    _, pairs = pair_table(panels)
    vmem = pl.BlockSpec(memory_space=pltpu.VMEM)

    beside = slots // columns
    far_back = jnp.einsum(
        "pjr,rk->pjk", far_factor, far_solution, precision=lax.Precision.HIGH
    )
    far_tiles = (
        far_back.reshape(panels // beside, beside, col_width, columns)
        .transpose(0, 2, 1, 3)
        .reshape(panels // beside, col_width, slots)
    )
    total = 3 * len(pairs) + 2 * panels + far_tiles.shape[0]
    tiles = jax.ShapeDtypeStruct((total, col_width, slots), jnp.float32)
    cols = width // col_width

    position = lax.axis_index("row") * slots + jnp.arange(slots)
    live = position[None, None, :] < anc_count[:, :, None]
    wanted = jnp.where(live, anc_rows, -1).reshape(-1)
    choice = (wanted[:, None] == jnp.arange(panels * width)[None, :]).astype(jnp.bfloat16)

    right_turned = right_sides.transpose(0, 1, 3, 2)
    slices, whole, tiles_all = pl.pallas_call(
        functools.partial(forward_kernel, peers, panels),
        out_shape=(
            jax.ShapeDtypeStruct((3, panels, columns, rows), jnp.float32),
            jax.ShapeDtypeStruct((panels, columns, width), jnp.float32),
            jax.ShapeDtypeStruct((cols,) + tiles.shape, jnp.float32),
        ),
        in_specs=[vmem, vmem, pl.BlockSpec(memory_space=pltpu.SMEM)] + [vmem] * 4,
        out_specs=(vmem, vmem, pl.BlockSpec(memory_space=pl.ANY)),
        scratch_shapes=[
            pltpu.VMEM((2 * panels, peers, 2, columns, rows), jnp.float32),
            pltpu.VMEM((peers, columns, panels * rows), jnp.float32),
            pltpu.VMEM((peers, columns, panels * rows), jnp.float32),
            pltpu.VMEM((cols,) + tiles.shape, jnp.float32),
            pltpu.SemaphoreType.DMA((2 * panels + 1, peers)),
            pltpu.SemaphoreType.DMA((2 * panels + 1, peers)),
            pltpu.SemaphoreType.DMA((6, cols, 1 + cols // LAYERS)),
            pltpu.SemaphoreType.DMA((6, cols)),
            pltpu.SemaphoreType.DMA,
        ],
        compiler_params=pltpu.CompilerParams(
            collective_id=0, has_side_effects=True, vmem_limit_bytes=VMEM_LIMIT
        ),
        name="forward",
    )(
        right_turned,
        diag_inverse,
        block_mask,
        sub_blocks.transpose(0, 1, 2, 4, 3),
        anc_values.transpose(0, 1, 3, 2),
        far_tiles,
        choice,
    )

    start = lax.axis_index("col") * col_width
    parent_cols = lax.dynamic_slice_in_dim(whole, start, col_width, 2)
    far_update = far_rhs - lax.psum_scatter(
        jnp.einsum("pjr,pkj->rk", far_factor, parent_cols, precision=lax.Precision.HIGH),
        "col",
        scatter_dimension=0,
        tiled=True,
    )

    turned = pl.pallas_call(
        functools.partial(backward_kernel, peers, panels),
        out_shape=jax.ShapeDtypeStruct((3, panels, columns, rows), jnp.float32),
        in_specs=[vmem] * 4,
        out_specs=vmem,
        scratch_shapes=[
            pltpu.VMEM((2 * panels, peers, 2, columns, rows), jnp.float32),
            pltpu.VMEM((2 * panels, peers, 2, columns, rows), jnp.float32),
            pltpu.VMEM((2 * panels, peers, 2, columns, rows), jnp.float32),
            pltpu.VMEM((peers, columns, rows), jnp.float32),
            pltpu.SemaphoreType.DMA((4 * panels, peers)),
            pltpu.SemaphoreType.DMA((4 * panels, peers)),
        ],
        compiler_params=pltpu.CompilerParams(
            collective_id=1, has_side_effects=True, vmem_limit_bytes=VMEM_LIMIT
        ),
        name="backward",
    )(slices, diag_inverse, tiles_all, choice)
    return (slices.transpose(0, 1, 3, 2), turned.transpose(0, 1, 3, 2), far_update)


def solution(mesh):
    in_specs = (
        P(None, None, "row", None),
        P(),
        P(None, None, None, "row", "col"),
        P(),
        P(None, None, "row", "col"),
        P(None, None, "row"),
        P(),
        P(None, "col", "row"),
        P(("row", "col"), None),
        P("row", None),
    )
    out_specs = (P(None, None, "row", None), P(None, None, "row", None), P(("row", "col"), None))
    return jax.shard_map(
        functools.partial(on_device, mesh.shape["row"]),
        mesh=mesh,
        in_specs=in_specs,
        out_specs=out_specs,
        check_vma=False,
    )
```
